128 devices in a mesh: seq: 8 (over y_hi, z), fsdp: 16 (over x, y_lo, core).
Axes of the slice: x: 4, y: 4 (y_hi: 2, y_lo: 2; y = y_hi * 2 + y_lo), z: 4, core: 2. Of those that a mesh axis runs over, the one named last changes fastest.
Arguments:
- queries: bfloat16 [32, 512, 8192], P('fsdp', None, 'seq'), may hold values from -48 to 48
- d_out: bfloat16 [32, 512, 8192], P('fsdp', None, 'seq'), may hold values from -12 to 12
- keys_values: bfloat16 [32, 512, 2048], P('fsdp', None, 'seq'), may hold values from -4.5 to 4.5
- lengths: int32 [32], P('fsdp'), may hold values from 1 to 512, 5461 in all
- w_kv: bfloat16 [8192, 2048], P('fsdp'), may hold values from -0.125 to 0.125
Outputs:
- d_queries: bfloat16 [32, 512, 8192], P('fsdp', 'seq')
- d_hidden: bfloat16 [32, 512, 8192], P('fsdp', 'seq')
The draws below stay inside these ranges and needn't reach their ends.
All inputs are finite; a program needn't handle non-finite values. No bound on the sum of `lengths` on one device may be relied on, other than what follows from the above.
Results may differ from the reference program's by a relative error of at most 0.009.
Values may be sent and summed in bfloat16 or wider, within the bound.
No kernel may reach another device: no remote copies, remote signals or barrier semaphores. Data moves between devices by JAX's collectives and lax.ppermute only.
A program may use at most 128 MiB of HBM per device.

```python
import math
import jax
import jax.numpy as jnp
import numpy as np
from jax import lax

D = 8192
H = 64
KVH = 8
HD = 128
L = 512
R = 32
N_SEQ = 8


def draw_saved(key):
    folded = jax.random.fold_in(key, 4242)
    seed_query, seed_key, seed_value = jax.random.split(folded, 3)
    query_shape = (R, L, H * HD)
    key_shape = (R, L, KVH * HD)
    query_draw = jnp.clip(jax.random.normal(seed_query, query_shape, jnp.float32), -4.5, 4.5)
    key_draw = jnp.clip(jax.random.normal(seed_key, key_shape, jnp.float32), -4.5, 4.5)
    value_draw = jnp.clip(jax.random.normal(seed_value, key_shape, jnp.float32), -4.5, 4.5)
    return (query_draw, jnp.concatenate([key_draw, value_draw], axis=2))


def draw_queries(key, part):
    return draw_saved(key)[0].astype(jnp.bfloat16)


def draw_keys_values(key, part):
    return draw_saved(key)[1].astype(jnp.bfloat16)


def block_levels(stream_key, shape, shards, least, high):
    level, own = 1.0, jax.random.fold_in(stream_key, 6)
    for axis_at, parts in shards:
        draws = jnp.exp(jax.random.uniform(jax.random.fold_in(own, axis_at), (parts,), jnp.float32, least / len(shards), high / len(shards)))
        level = level * jnp.repeat(draws, shape[axis_at] // parts).reshape([-1 if axis == axis_at else 1 for axis in range(len(shape))])
    return level


def length_profile(number_of, total, limit, lean):
    weights = [(1 << 20) // math.isqrt(grade ** lean) + 1 for grade in range(2, number_of + 1)]
    rest, counts = total - limit - (number_of - 1), [1] * (number_of - 1)
    while rest > 0:
        movable = [i for i in range(number_of - 1) if counts[i] < limit]
        mass, budget = sum([weights[i] for i in movable]), rest
        for i in movable:
            extra = min(limit - counts[i], max(1, budget * weights[i] // mass), rest)
            counts[i] = counts[i] + extra
            rest = rest - extra
    return np.array([limit] + counts)


def ragged_sizes(key, number_of, total, most, skew):
    if number_of == 2:
        one = jax.random.randint(key, (), max(1, total - most), min(most, total - 1) + 1)
        return jnp.stack([one, total - one])
    sizes = jnp.asarray(length_profile(number_of, total, most, skew), jnp.int32)
    couples = (number_of - 1) // 2
    donor, taker = sizes[1:1 + 2 * couples:2], sizes[2:2 + 2 * couples:2]
    margin = jnp.minimum(donor - 1, most - taker)
    shifted = jax.random.randint(jax.random.fold_in(key, 1), (couples,), 0, 1 << 20) % (margin + 1)
    sizes = sizes.at[1:1 + 2 * couples:2].set(donor - shifted).at[2:2 + 2 * couples:2].set(taker + shifted)
    return sizes[jax.random.permutation(jax.random.fold_in(key, 2), number_of)]


def scatter_about(own_key, shape, deviation, most, shards=(), kind=jnp.bfloat16):
    entries = deviation * jax.random.normal(own_key, shape, jnp.float32)
    if shards:
        entries = entries * block_levels(own_key, shape, shards, -0.22, 0.18)
    return jnp.clip(entries, -most, most).astype(kind)


def setup_inputs(seed: int = 0) -> dict:
    key_list = jax.random.split(jax.random.key(seed), 6)
    return {
        "queries": draw_queries(jax.random.fold_in(key_list[5], 71), 0),
        "d_out": scatter_about(key_list[1], (R, L, H * HD), 2.0, 12.0, ((0, 16), (2, 8))),
        "keys_values": draw_keys_values(jax.random.fold_in(key_list[5], 71), 0),
        "lengths": ragged_sizes(key_list[3], R, R * L // 3, L, 2).astype(jnp.int32),
        "w_kv": scatter_about(key_list[4], (D, 2 * KVH * HD), (2 * KVH * HD) ** -0.5, 0.125, ((0, 16),)),
    }


def rollout_terms(query_rows, dout_rows, kv_rows, length):
    score_scale = 1.0 / math.sqrt(HD)
    group_size = H // KVH
    shard_rows = L // N_SEQ
    query_split = query_rows.astype(jnp.float32).reshape(L, KVH, group_size, HD)
    grad_split = dout_rows.astype(jnp.float32).reshape(L, KVH, group_size, HD)
    key_split = kv_rows[:, :KVH * HD].astype(jnp.float32).reshape(L, KVH, HD)
    value_split = kv_rows[:, KVH * HD:].astype(jnp.float32).reshape(L, KVH, HD)
    scores = jnp.einsum('icgd,jcd->cgij', query_split, key_split) * score_scale
    positions = jnp.arange(L, dtype=jnp.int32)
    allowed = (positions[None, :] <= positions[:, None]) & (positions[:, None] < length)
    masked = jnp.where(allowed, scores, -1e+30)
    largest = lax.optimization_barrier(jnp.max(masked, axis=-1, keepdims=True))
    numer = jnp.where(allowed, jnp.exp(masked - largest), 0.0)
    totals = lax.optimization_barrier(jnp.sum(numer, axis=-1, keepdims=True))
    probability = numer / jnp.maximum(totals, 1.0)
    prob_half = lax.optimization_barrier(probability.astype(jnp.bfloat16)).astype(jnp.float32)
    output_rec = jnp.einsum('cgij,jcd->icgd', prob_half, value_split)
    row_dot = lax.optimization_barrier(jnp.sum(grad_split * output_rec, axis=-1))
    grad_prob = jnp.einsum('icgd,jcd->cgij', grad_split, value_split)
    grad_score = probability * (grad_prob - jnp.transpose(row_dot, (1, 2, 0))[..., None])
    grad_half = lax.optimization_barrier(grad_score.astype(jnp.bfloat16)).astype(jnp.float32)
    grad_query = (score_scale * jnp.einsum('cgij,jcd->icgd', grad_half, key_split)).astype(jnp.bfloat16)
    grad_query = grad_query.reshape(L, H * HD)
    grad_shards = grad_half.reshape(KVH, group_size, N_SEQ, shard_rows, L)
    prob_shards = prob_half.reshape(KVH, group_size, N_SEQ, shard_rows, L)
    query_shards = query_split.reshape(N_SEQ, shard_rows, KVH, group_size, HD)
    dout_shards = grad_split.reshape(N_SEQ, shard_rows, KVH, group_size, HD)
    grad_key = score_scale * jnp.einsum('cgsij,sicgd->sjcd', grad_shards, query_shards)
    grad_value = jnp.einsum('cgsij,sicgd->sjcd', prob_shards, dout_shards)
    partial_value = jnp.concatenate([grad_key.reshape(N_SEQ, L, KVH * HD), grad_value.reshape(N_SEQ, L, KVH * HD)], axis=-1)
    partial_value = lax.optimization_barrier(partial_value.astype(jnp.bfloat16)).astype(jnp.float32)
    grad_kv = lax.optimization_barrier(jnp.sum(partial_value, axis=0)).astype(jnp.bfloat16)
    return (grad_query, grad_kv)

def reference(queries, d_out, keys_values, lengths, w_kv):
    d_queries, grad_kv = lax.map(lambda members: rollout_terms(*members), (queries, d_out, keys_values, lengths))
    flat = grad_kv.reshape(R * L, 2 * KVH * HD)
    d_hidden = jnp.dot(flat, w_kv.T, preferred_element_type=jnp.float32).astype(jnp.bfloat16)
    return (d_queries, d_hidden.reshape(R, L, D))
```

```python
import math

import jax
import jax.numpy as jnp
from jax import lax
from jax.experimental import pallas as pl
from jax.experimental.pallas import tpu as pltpu
from jax.sharding import PartitionSpec as P

HD = 128
GROUP = 8
N_SEQ = 8
BAND = 64
ROWS = N_SEQ * BAND
BI = 256
HEADS_A_STEP = 2
SCALE = 1.0 / math.sqrt(HD)
EXP2_SCALE = SCALE * math.log2(math.e)


def dot(a, b, ca, cb):
    return lax.dot_general(a, b, (((ca,), (cb,)), ((), ())), preferred_element_type=jnp.float32)


def attention_kernel(len_ref, odd_ref, q_ref, do_ref, a_ref, b_ref, dq_ref, gkv_ref, k_s, v_s, kt_s, dk_s, dv_s):
    step = pl.program_id(1)
    live = len_ref[pl.program_id(0)]

    @pl.when(step == 0)
    def _():
        @pl.when(odd_ref[0] == 0)
        def _():
            k_s[...] = a_ref[0]
            v_s[...] = b_ref[0]

        @pl.when(odd_ref[0] != 0)
        def _():
            k_s[...] = b_ref[0]
            v_s[...] = a_ref[0]

        kt_s[...] = k_s[...].T
        dk_s[...] = jnp.zeros_like(dk_s)
        dv_s[...] = jnp.zeros_like(dv_s)

    for block in range(ROWS // BI):
        lo, hi = block * BI, (block + 1) * BI
        bands = slice(lo // BAND, hi // BAND)

        @pl.when(live > lo)
        def _():
            below = lax.broadcasted_iota(jnp.int32, (BI, BI), 0) <= lax.broadcasted_iota(jnp.int32, (BI, BI), 1)
            alive = lo + lax.broadcasted_iota(jnp.int32, (1, BI), 1) < live
            for head in range(HEADS_A_STEP):
                cols = slice(head * HD, (head + 1) * HD)
                q = q_ref[0, lo:hi, cols]
                do = do_ref[0, lo:hi, cols]
                spans = ([slice(0, lo)] if lo else []) + [slice(lo, hi)]
                scores = [dot(k_s[span, :], q, 1, 1) for span in spans]
                grad_prob = [dot(v_s[span, :], do, 1, 1) for span in spans]
                scores[-1] = jnp.where(below, scores[-1], -1e30)
                largest = scores[-1].max(0, keepdims=True)
                if lo:
                    largest = jnp.maximum(largest, scores[0].max(0, keepdims=True))
                numer = [jnp.exp2((s - largest) * EXP2_SCALE) for s in scores]
                total = sum(n.sum(0, keepdims=True) for n in numer)
                inverse = jnp.where(alive, 1.0 / jnp.maximum(total, 1.0), 0.0)
                row_dot = sum((n * g).sum(0, keepdims=True) for n, g in zip(numer, grad_prob)) * inverse
                dqt = None
                for span, n, g in zip(spans, numer, grad_prob):
                    prob = n * inverse
                    grad_score = (prob * (g - row_dot)).astype(jnp.bfloat16)
                    dv_s[span, :] += dot(prob.astype(jnp.bfloat16), do, 1, 0)
                    dk_s[span, :] += dot(grad_score, q, 1, 0)
                    part = dot(kt_s[:, span], grad_score, 1, 0)
                    dqt = part if dqt is None else dqt + part
                dq = (dqt * SCALE).T.astype(jnp.bfloat16)
                dq_ref[bands, 0, :, cols] = dq.reshape(BI // BAND, BAND, HD)

        @pl.when(live <= lo)
        def _():
            dq_ref[bands] = jnp.zeros((BI // BAND, 1, BAND, HEADS_A_STEP * HD), jnp.bfloat16)

    @pl.when(step == pl.num_programs(1) - 1)
    def _():
        gkv_ref[:, 0, :, :HD] = (dk_s[...] * SCALE).astype(jnp.bfloat16).reshape(N_SEQ, BAND, HD)
        gkv_ref[:, 0, :, HD:] = dv_s[...].astype(jnp.bfloat16).reshape(N_SEQ, BAND, HD)


def attention(lengths, odd, queries, d_out, a, b):
    rollouts = queries.shape[0]
    wide = HEADS_A_STEP * HD
    rows = pl.BlockSpec((1, ROWS, wide), lambda r, h, *_: (r, 0, h))
    whole = pl.BlockSpec((1, ROWS, HD), lambda r, h, *_: (r, 0, 0))
    return pl.pallas_call(
        attention_kernel,
        out_shape=(
            jax.ShapeDtypeStruct((N_SEQ, rollouts, BAND, GROUP * HD), jnp.bfloat16),
            jax.ShapeDtypeStruct((N_SEQ, rollouts, BAND, 2 * HD), jnp.bfloat16),
        ),
        grid_spec=pltpu.PrefetchScalarGridSpec(
            num_scalar_prefetch=2,
            grid=(rollouts, GROUP // HEADS_A_STEP),
            in_specs=[rows, rows, whole, whole],
            out_specs=[
                pl.BlockSpec((N_SEQ, 1, BAND, wide), lambda r, h, *_: (0, r, 0, h)),
                pl.BlockSpec((N_SEQ, 1, BAND, 2 * HD), lambda r, h, *_: (0, r, 0, 0)),
            ],
            scratch_shapes=[
                pltpu.VMEM((ROWS, HD), jnp.bfloat16),
                pltpu.VMEM((ROWS, HD), jnp.bfloat16),
                pltpu.VMEM((HD, ROWS), jnp.bfloat16),
                pltpu.VMEM((ROWS, HD), jnp.float32),
                pltpu.VMEM((ROWS, HD), jnp.float32),
            ],
        ),
        name="attention",
    )(lengths, odd, queries, d_out, a, b)


def project_kernel(at_ref, g0, g1, g2, g3, w0, w1, w2, w3, o_ref, w_s, sems):
    weights = (w0, w1, w2, w3)
    copies = [pltpu.make_async_copy(w, w_s.at[i], sems.at[i]) for i, w in enumerate(weights)]
    for copy in copies:
        copy.start()
    x, q = at_ref[0], at_ref[1]
    steps = (0, 3, 1, 2)
    for i, copy in enumerate(copies):
        copy.wait()
        col = pl.multiple_of((q ^ i) * w_s.shape[1], w_s.shape[1])
        for step, g in zip(steps, (g0, g1, g2, g3)):
            out = dot(g[...], w_s[i], 1, 1).astype(jnp.bfloat16)
            o_ref[(x + step) % 4, :, pl.ds(col, w_s.shape[1])] = out


def project(at, pieces, weights):
    rows, depth = pieces[0].shape
    shard = weights[0].shape[0]
    vmem = pl.BlockSpec(memory_space=pltpu.VMEM)
    return pl.pallas_call(
        project_kernel,
        out_shape=jax.ShapeDtypeStruct((4, rows, 4 * shard), jnp.bfloat16),
        in_specs=[pl.BlockSpec(memory_space=pltpu.SMEM)] + [vmem] * 4 + [pl.BlockSpec(memory_space=pl.ANY)] * 4,
        out_specs=vmem,
        scratch_shapes=[pltpu.VMEM((4, shard, depth), jnp.bfloat16), pltpu.SemaphoreType.DMA((4,))],
        name="project",
    )(at, *pieces, *weights)


X_UP = [(f, (f + 4) % 16) for f in range(16)]
X_DOWN = [(f, (f + 12) % 16) for f in range(16)]
X_GROUPS = [[x * 4 + q for x in range(4)] for q in range(4)]
CORE = [(f, f ^ 1) for f in range(16)]
NEAR = [(f, f ^ 2) for f in range(16)]
FIRST = [(t, 2 * t) for t in range(4)] + [(4 + t, 2 * t + 1) for t in range(4)]
SECOND = [(t, 2 * t + 1) for t in range(4)] + [(4 + t, 2 * t) for t in range(4)]


def local(queries, d_out, keys_values, lengths, w_kv):
    seq = lax.axis_index("seq")
    fsdp = lax.axis_index("fsdp")
    rollouts = queries.shape[0]
    low, high = keys_values[:, :, :HD], keys_values[:, :, HD:]
    holds_keys = seq < 4
    a = lax.ppermute(jnp.where(holds_keys, low, high), "seq", FIRST)
    b = lax.ppermute(jnp.where(holds_keys, high, low), "seq", SECOND)
    w_near = lax.ppermute(w_kv, "fsdp", NEAR)
    w_core = lax.ppermute(w_kv, "fsdp", CORE)
    w_far = lax.ppermute(w_near, "fsdp", CORE)
    odd = (seq % 2).astype(jnp.int32).reshape(1)
    dq, gkv = attention(lengths, odd, queries, d_out, a, b)

    gkv = lax.all_to_all(gkv, "seq", split_axis=0, concat_axis=0, tiled=True)
    dq = lax.all_to_all(dq, "seq", split_axis=0, concat_axis=0, tiled=True)
    rows = rollouts * BAND
    g = gkv.reshape(N_SEQ, rows, 2, HD).transpose(1, 2, 0, 3).reshape(rows, 2 * N_SEQ * HD)
    from_down = lax.ppermute(g, "fsdp", X_UP)
    from_up = lax.ppermute(g, "fsdp", X_DOWN)
    half = rows // 2
    across = jnp.concatenate(
        [lax.ppermute(from_down[:half], "fsdp", X_UP), lax.ppermute(from_up[half:], "fsdp", X_DOWN)], axis=0
    )
    at = jnp.stack([fsdp // 4, fsdp % 4]).astype(jnp.int32)
    out = project(at, (g, from_down, from_up, across), (w_kv, w_core, w_near, w_far))
    out = lax.all_to_all(out, "fsdp", split_axis=0, concat_axis=0, axis_index_groups=X_GROUPS, tiled=True)
    d_hidden = out.reshape(4, rollouts, BAND, -1).transpose(1, 2, 0, 3).reshape(rollouts, BAND, -1)
    d_queries = dq.transpose(1, 2, 0, 3).reshape(rollouts, BAND, -1)
    return d_queries, d_hidden


def solution(mesh):
    in_specs = (
        P("fsdp", None, "seq"),
        P("fsdp", None, "seq"),
        P("fsdp", None, "seq"),
        P("fsdp"),
        P("fsdp", None),
    )
    out_specs = (P("fsdp", "seq", None), P("fsdp", "seq", None))
    return jax.shard_map(local, mesh=mesh, in_specs=in_specs, out_specs=out_specs, check_vma=False)
```

```python
import math

import jax
import jax.numpy as jnp
from jax import lax
from jax.experimental import pallas as pl
from jax.experimental.pallas import tpu as pltpu
from jax.sharding import PartitionSpec as P


HD = 128
GROUP = 8
N_SEQ = 8
BAND = 64
ROWS = N_SEQ * BAND
BI = 256
HEADS_A_STEP = 2
SCALE = 1.0 / math.sqrt(HD)
EXP2_SCALE = SCALE * math.log2(math.e)


def dot(a, b, ca, cb):
    return lax.dot_general(a, b, (((ca,), (cb,)), ((), ())), preferred_element_type=jnp.float32)


def attention_kernel(len_ref, odd_ref, q_ref, do_ref, a_ref, b_ref, dq_ref, gkv_ref, k_s, v_s, kt_s, dk_s, dv_s):
    step = pl.program_id(1)
    live = len_ref[pl.program_id(0)]

    @pl.when(step == 0)
    def _():
        @pl.when(odd_ref[0] == 0)
        def _():
            k_s[...] = a_ref[0]
            v_s[...] = b_ref[0]

        @pl.when(odd_ref[0] != 0)
        def _():
            k_s[...] = b_ref[0]
            v_s[...] = a_ref[0]

        kt_s[...] = k_s[...].T
        dk_s[...] = jnp.zeros_like(dk_s)
        dv_s[...] = jnp.zeros_like(dv_s)

    for block in range(ROWS // BI):
        lo, hi = block * BI, (block + 1) * BI
        bands = slice(lo // BAND, hi // BAND)

        @pl.when(live > lo)
        def _():
            below = lax.broadcasted_iota(jnp.int32, (BI, BI), 0) <= lax.broadcasted_iota(jnp.int32, (BI, BI), 1)
            alive = lo + lax.broadcasted_iota(jnp.int32, (1, BI), 1) < live
            for head in range(HEADS_A_STEP):
                cols = slice(head * HD, (head + 1) * HD)
                q = q_ref[0, lo:hi, cols]
                do = do_ref[0, lo:hi, cols]
                spans = ([slice(0, lo)] if lo else []) + [slice(lo, hi)]
                scores = [dot(k_s[span, :], q, 1, 1) for span in spans]
                grad_prob = [dot(v_s[span, :], do, 1, 1) for span in spans]
                scores[-1] = jnp.where(below, scores[-1], -1e30)
                largest = scores[-1].max(0, keepdims=True)
                if lo:
                    largest = jnp.maximum(largest, scores[0].max(0, keepdims=True))
                numer = [jnp.exp2((s - largest) * EXP2_SCALE) for s in scores]
                total = sum(n.sum(0, keepdims=True) for n in numer)
                inverse = jnp.where(alive, 1.0 / jnp.maximum(total, 1.0), 0.0)
                row_dot = sum((n * g).sum(0, keepdims=True) for n, g in zip(numer, grad_prob)) * inverse
                dqt = None
                for span, n, g in zip(spans, numer, grad_prob):
                    prob = n * inverse
                    grad_score = (prob * (g - row_dot)).astype(jnp.bfloat16)
                    dv_s[span, :] += dot(prob.astype(jnp.bfloat16), do, 1, 0)
                    dk_s[span, :] += dot(grad_score, q, 1, 0)
                    part = dot(kt_s[:, span], grad_score, 1, 0)
                    dqt = part if dqt is None else dqt + part
                dq = (dqt * SCALE).T.astype(jnp.bfloat16)
                dq_ref[bands, 0, :, cols] = dq.reshape(BI // BAND, BAND, HD)

        @pl.when(live <= lo)
        def _():
            dq_ref[bands] = jnp.zeros((BI // BAND, 1, BAND, HEADS_A_STEP * HD), jnp.bfloat16)

    @pl.when(step == pl.num_programs(1) - 1)
    def _():
        gkv_ref[:, 0, :, :HD] = (dk_s[...] * SCALE).astype(jnp.bfloat16).reshape(N_SEQ, BAND, HD)
        gkv_ref[:, 0, :, HD:] = dv_s[...].astype(jnp.bfloat16).reshape(N_SEQ, BAND, HD)


def attention(lengths, odd, queries, d_out, a, b):
    rollouts = queries.shape[0]
    wide = HEADS_A_STEP * HD
    rows = pl.BlockSpec((1, ROWS, wide), lambda r, h, *_: (r, 0, h))
    whole = pl.BlockSpec((1, ROWS, HD), lambda r, h, *_: (r, 0, 0))
    return pl.pallas_call(
        attention_kernel,
        out_shape=(
            jax.ShapeDtypeStruct((N_SEQ, rollouts, BAND, GROUP * HD), jnp.bfloat16),
            jax.ShapeDtypeStruct((N_SEQ, rollouts, BAND, 2 * HD), jnp.bfloat16),
        ),
        grid_spec=pltpu.PrefetchScalarGridSpec(
            num_scalar_prefetch=2,
            grid=(rollouts, GROUP // HEADS_A_STEP),
            in_specs=[rows, rows, whole, whole],
            out_specs=[
                pl.BlockSpec((N_SEQ, 1, BAND, wide), lambda r, h, *_: (0, r, 0, h)),
                pl.BlockSpec((N_SEQ, 1, BAND, 2 * HD), lambda r, h, *_: (0, r, 0, 0)),
            ],
            scratch_shapes=[
                pltpu.VMEM((ROWS, HD), jnp.bfloat16),
                pltpu.VMEM((ROWS, HD), jnp.bfloat16),
                pltpu.VMEM((HD, ROWS), jnp.bfloat16),
                pltpu.VMEM((ROWS, HD), jnp.float32),
                pltpu.VMEM((ROWS, HD), jnp.float32),
            ],
        ),
        name="attention",
    )(lengths, odd, queries, d_out, a, b)


def project_kernel(*refs):
    gs, outs, (g_s, w_s, sems) = refs[:4], refs[-7:-3], refs[-3:]
    weights = refs[4:-7]
    starts = [sum(w.shape[0] for w in weights[:i]) for i in range(len(weights) + 1)]
    spans = [slice(a, b) for a, b in zip(starts, starts[1:])]
    copies = [pltpu.make_async_copy(w, w_s.at[span], sems.at[i]) for i, (w, span) in enumerate(zip(weights, spans))]
    for copy in copies:
        copy.start()
    rows = gs[0].shape[0]
    for i, g in enumerate(gs):
        g_s[i * rows : (i + 1) * rows, :] = g[...]
    for copy, span in zip(copies, spans):
        copy.wait()
        out = dot(g_s[...], w_s[span], 1, 1).astype(jnp.bfloat16)
        for k, o in enumerate(outs):
            o[:, span] = out[k * rows : (k + 1) * rows]


def project(pieces, weights):
    rows, depth = pieces[0].shape
    cols = sum(w.shape[0] for w in weights)
    vmem = pl.BlockSpec(memory_space=pltpu.VMEM)
    return pl.pallas_call(
        project_kernel,
        out_shape=(jax.ShapeDtypeStruct((rows, cols), jnp.bfloat16),) * 4,
        in_specs=[vmem] * 4 + [pl.BlockSpec(memory_space=pl.ANY)] * len(weights),
        out_specs=[vmem] * 4,
        scratch_shapes=[
            pltpu.VMEM((4 * rows, depth), jnp.bfloat16),
            pltpu.VMEM((cols, depth), jnp.bfloat16),
            pltpu.SemaphoreType.DMA((len(weights),)),
        ],
        name="project",
    )(*pieces, *weights)


def assemble_kernel(at_ref, *refs):
    x, q = at_ref[0], at_ref[1]
    o_ref = refs[-1]
    for chunk, steps in enumerate(STEPS):
        for k in range(4):
            block = refs[4 * chunk + k]
            shard = block.shape[1] // 2
            for i, step in enumerate(steps):
                col = pl.multiple_of(((x + step) % 4 * 4 + (q ^ k)) * shard, shard)
                o_ref[:, pl.ds(col, shard)] = block[:, i * shard : (i + 1) * shard]


def assemble(at, blocks):
    rows, cols = blocks[0].shape
    vmem = pl.BlockSpec(memory_space=pltpu.VMEM)
    return pl.pallas_call(
        assemble_kernel,
        out_shape=jax.ShapeDtypeStruct((rows, 8 * cols), jnp.bfloat16),
        in_specs=[pl.BlockSpec(memory_space=pltpu.SMEM)] + [vmem] * 8,
        out_specs=vmem,
        name="assemble",
    )(at, *blocks)


X_UP = [(f, (f + 4) % 16) for f in range(16)]
X_DOWN = [(f, (f + 12) % 16) for f in range(16)]
CORE = [(f, f ^ 1) for f in range(16)]
NEAR = [(f, f ^ 2) for f in range(16)]
DIAGONAL = [(f, f ^ 3) for f in range(16)]
STEPS = ((0, 3), (1, 2))
FIRST = [(t, 2 * t) for t in range(4)] + [(4 + t, 2 * t + 1) for t in range(4)]
SECOND = [(t, 2 * t + 1) for t in range(4)] + [(4 + t, 2 * t) for t in range(4)]


def body(queries, d_out, keys_values, lengths, w_kv):
    seq = lax.axis_index("seq")
    fsdp = lax.axis_index("fsdp")
    rollouts = queries.shape[0]
    low, high = keys_values[:, :, :HD], keys_values[:, :, HD:]
    holds_keys = seq < 4
    a = lax.ppermute(jnp.where(holds_keys, low, high), "seq", FIRST)
    b = lax.ppermute(jnp.where(holds_keys, high, low), "seq", SECOND)
    half = w_kv.shape[0] // 2
    w0, w1 = w_kv[:half], w_kv[half:]
    up0 = lax.ppermute(w0, "fsdp", X_UP)
    down1 = lax.ppermute(w1, "fsdp", X_DOWN)
    up1 = lax.ppermute(w1, "fsdp", X_UP)
    down0 = lax.ppermute(w0, "fsdp", X_DOWN)
    across0 = lax.ppermute(up0, "fsdp", X_UP)
    across1 = lax.ppermute(down1, "fsdp", X_DOWN)
    odd = (seq % 2).astype(jnp.int32).reshape(1)
    at = jnp.stack([fsdp // 4, fsdp % 4]).astype(jnp.int32)
    dq, gkv = attention(lengths, odd, queries, d_out, a, b)
    gkv = lax.all_to_all(gkv, "seq", split_axis=0, concat_axis=0, tiled=True)
    dq = lax.all_to_all(dq, "seq", split_axis=0, concat_axis=0, tiled=True)
    rows = rollouts * BAND
    g = gkv.reshape(N_SEQ, rows, 2, HD).transpose(1, 2, 0, 3).reshape(rows, 2 * N_SEQ * HD)
    g_near = lax.ppermute(g, "fsdp", NEAR)
    g_core = lax.ppermute(g, "fsdp", CORE)
    g_far = lax.ppermute(g_near, "fsdp", CORE)
    pieces = (g, g_core, g_near, g_far)
    blocks = []
    for weights in ((w_kv, up0, up1), (down0, down1, across0, across1)):
        own, core, near, far = project(pieces, weights)
        near = lax.ppermute(near, "fsdp", NEAR)
        far = lax.ppermute(far, "fsdp", DIAGONAL)
        core = lax.ppermute(core, "fsdp", CORE)
        blocks += [own, core, near, far]
    d_hidden = assemble(at, blocks).reshape(rollouts, BAND, -1)
    d_queries = dq.transpose(1, 2, 0, 3).reshape(rollouts, BAND, -1)
    return d_queries, d_hidden


def solution(mesh):
    in_specs = (
        P("fsdp", None, "seq"),
        P("fsdp", None, "seq"),
        P("fsdp", None, "seq"),
        P("fsdp"),
        P("fsdp", None),
    )
    out_specs = (P("fsdp", "seq", None), P("fsdp", "seq", None))
    return jax.shard_map(body, mesh=mesh, in_specs=in_specs, out_specs=out_specs, check_vma=False)
```

```python
import math

import jax
import jax.numpy as jnp
from jax import lax
from jax.experimental import pallas as pl
from jax.experimental.pallas import tpu as pltpu
from jax.sharding import PartitionSpec as P


HD = 128
GROUP = 8
N_SEQ = 8
BAND = 64
ROWS = N_SEQ * BAND
BI = 128
HEADS_A_STEP = 8
SCALE = 1.0 / math.sqrt(HD)
EXP2_SCALE = SCALE * math.log2(math.e)


def dot(a, b, ca, cb):
    return lax.dot_general(a, b, (((ca,), (cb,)), ((), ())), preferred_element_type=jnp.float32)


def attention_kernel(len_ref, odd_ref, q_ref, do_ref, a_ref, b_ref, dq_ref, gkv_ref, k_s, v_s, kt_s, dk_s, dv_s):
    step = pl.program_id(1)
    live = len_ref[pl.program_id(0)]

    @pl.when(step == 0)
    def _():
        @pl.when(odd_ref[0] == 0)
        def _():
            k_s[...] = a_ref[0]
            v_s[...] = b_ref[0]

        @pl.when(odd_ref[0] != 0)
        def _():
            k_s[...] = b_ref[0]
            v_s[...] = a_ref[0]

        kt_s[...] = k_s[...].T
        dk_s[...] = jnp.zeros_like(dk_s)
        dv_s[...] = jnp.zeros_like(dv_s)

    def heads_of(ref, lo, hi):
        parts = [ref[0, lo:hi, head * HD : (head + 1) * HD] for head in range(HEADS_A_STEP)]
        return jnp.concatenate(parts, axis=0)

    for block in range(ROWS // BI):
        lo, hi = block * BI, (block + 1) * BI
        bands = slice(lo // BAND, hi // BAND)

        @pl.when(live > lo)
        def _():
            wide = HEADS_A_STEP * BI
            row = lax.broadcasted_iota(jnp.int32, (1, wide), 1) % BI
            below = lax.broadcasted_iota(jnp.int32, (BI, wide), 0) <= row
            q, do = heads_of(q_ref, lo, hi), heads_of(do_ref, lo, hi)
            spans = ([slice(0, lo)] if lo else []) + [slice(lo, hi)]
            scores = [dot(k_s[span, :], q, 1, 1) for span in spans]
            grad_prob = [dot(v_s[span, :], do, 1, 1) for span in spans]
            scores[-1] = jnp.where(below, scores[-1], -1e30)
            largest = scores[-1].max(0, keepdims=True)
            if lo:
                largest = jnp.maximum(largest, scores[0].max(0, keepdims=True))
            numer = [jnp.exp2((s - largest) * EXP2_SCALE) for s in scores]
            total = sum(n.sum(0, keepdims=True) for n in numer)
            inverse = jnp.where(lo + row < live, 1.0 / jnp.maximum(total, 1.0), 0.0)
            row_dot = sum((n * g).sum(0, keepdims=True) for n, g in zip(numer, grad_prob)) * inverse
            dqt = None
            for span, n, g in zip(spans, numer, grad_prob):
                prob = n * inverse
                grad_score = (prob * (g - row_dot)).astype(jnp.bfloat16)
                dv_s[span, :] += dot(prob.astype(jnp.bfloat16), do, 1, 0)
                dk_s[span, :] += dot(grad_score, q, 1, 0)
                part = dot(kt_s[:, span], grad_score, 1, 0)
                dqt = part if dqt is None else dqt + part
            dqt = dqt * SCALE
            for head in range(HEADS_A_STEP):
                dq = dqt[:, head * BI : (head + 1) * BI].T.astype(jnp.bfloat16)
                dq_ref[bands, 0, :, head * HD : (head + 1) * HD] = dq.reshape(BI // BAND, BAND, HD)

        @pl.when(live <= lo)
        def _():
            dq_ref[bands] = jnp.zeros((BI // BAND, 1, BAND, HEADS_A_STEP * HD), jnp.bfloat16)

    @pl.when(step == pl.num_programs(1) - 1)
    def _():
        gkv_ref[:, 0, :, :HD] = (dk_s[...] * SCALE).astype(jnp.bfloat16).reshape(N_SEQ, BAND, HD)
        gkv_ref[:, 0, :, HD:] = dv_s[...].astype(jnp.bfloat16).reshape(N_SEQ, BAND, HD)


def attention(lengths, odd, queries, d_out, a, b):
    rollouts = queries.shape[0]
    wide = HEADS_A_STEP * HD
    rows = pl.BlockSpec((1, ROWS, wide), lambda r, h, *_: (r, 0, h))
    whole = pl.BlockSpec((1, ROWS, HD), lambda r, h, *_: (r, 0, 0))
    return pl.pallas_call(
        attention_kernel,
        out_shape=(
            jax.ShapeDtypeStruct((N_SEQ, rollouts, BAND, GROUP * HD), jnp.bfloat16),
            jax.ShapeDtypeStruct((N_SEQ, rollouts, BAND, 2 * HD), jnp.bfloat16),
        ),
        grid_spec=pltpu.PrefetchScalarGridSpec(
            num_scalar_prefetch=2,
            grid=(rollouts, GROUP // HEADS_A_STEP),
            in_specs=[rows, rows, whole, whole],
            out_specs=[
                pl.BlockSpec((N_SEQ, 1, BAND, wide), lambda r, h, *_: (0, r, 0, h)),
                pl.BlockSpec((N_SEQ, 1, BAND, 2 * HD), lambda r, h, *_: (0, r, 0, 0)),
            ],
            scratch_shapes=[
                pltpu.VMEM((ROWS, HD), jnp.bfloat16),
                pltpu.VMEM((ROWS, HD), jnp.bfloat16),
                pltpu.VMEM((HD, ROWS), jnp.bfloat16),
                pltpu.VMEM((ROWS, HD), jnp.float32),
                pltpu.VMEM((ROWS, HD), jnp.float32),
            ],
        ),
        name="attention",
    )(lengths, odd, queries, d_out, a, b)


def project_kernel(*refs):
    gs, outs, (g_s, w_s, sems) = refs[:4], refs[-7:-3], refs[-3:]
    weights = refs[4:-7]
    rows = gs[0].shape[0]
    starts = [sum(w.shape[0] for w in weights[:i]) for i in range(len(weights) + 1)]
    spans = [slice(a, b) for a, b in zip(starts, starts[1:])]
    loads = [pltpu.make_async_copy(g, g_s.at[i * rows : (i + 1) * rows], sems.at[i]) for i, g in enumerate(gs)]
    copies = [pltpu.make_async_copy(w, w_s.at[span], sems.at[4 + i]) for i, (w, span) in enumerate(zip(weights, spans))]
    for copy in loads + copies:
        copy.start()
    for copy in loads:
        copy.wait()
    for copy, span in zip(copies, spans):
        copy.wait()
        out = dot(g_s[...], w_s[span], 1, 1).astype(jnp.bfloat16)
        for k, o in enumerate(outs):
            o[:, span] = out[k * rows : (k + 1) * rows]


def project(pieces, weights):
    rows, depth = pieces[0].shape
    cols = sum(w.shape[0] for w in weights)
    stay = pl.BlockSpec(memory_space=pl.ANY)
    return pl.pallas_call(
        project_kernel,
        out_shape=(jax.ShapeDtypeStruct((rows, cols), jnp.bfloat16),) * 4,
        in_specs=[stay] * (4 + len(weights)),
        out_specs=[pl.BlockSpec(memory_space=pltpu.VMEM)] * 4,
        scratch_shapes=[
            pltpu.VMEM((4 * rows, depth), jnp.bfloat16),
            pltpu.VMEM((cols, depth), jnp.bfloat16),
            pltpu.SemaphoreType.DMA((4 + len(weights),)),
        ],
        name="project",
    )(*pieces, *weights)


def assemble_kernel(at_ref, *refs):
    x, q = at_ref[0], at_ref[1]
    o_ref = refs[-1]
    for chunk, steps in enumerate(STEPS):
        for k in range(4):
            block = refs[4 * chunk + k]
            shard = block.shape[1] // len(steps)
            for i, step in enumerate(steps):
                col = pl.multiple_of(((x + step) % 4 * 4 + (q ^ k)) * shard, shard)
                o_ref[:, pl.ds(col, shard)] = block[:, i * shard : (i + 1) * shard]


def assemble(at, blocks):
    rows = blocks[0].shape[0]
    cols = sum(block.shape[1] for block in blocks)
    vmem = pl.BlockSpec(memory_space=pltpu.VMEM)
    return pl.pallas_call(
        assemble_kernel,
        out_shape=jax.ShapeDtypeStruct((rows, cols), jnp.bfloat16),
        in_specs=[pl.BlockSpec(memory_space=pltpu.SMEM)] + [vmem] * len(blocks),
        out_specs=vmem,
        name="assemble",
    )(at, *blocks)


X_UP = [(f, (f + 4) % 16) for f in range(16)]
X_DOWN = [(f, (f + 12) % 16) for f in range(16)]
CORE = [(f, f ^ 1) for f in range(16)]
NEAR = [(f, f ^ 2) for f in range(16)]
DIAGONAL = [(f, f ^ 3) for f in range(16)]
STEPS = ((0, 3, 1), (2,))
FIRST = [(t, 2 * t) for t in range(4)] + [(4 + t, 2 * t + 1) for t in range(4)]
SECOND = [(t, 2 * t + 1) for t in range(4)] + [(4 + t, 2 * t) for t in range(4)]


def body(queries, d_out, keys_values, lengths, w_kv):
    seq = lax.axis_index("seq")
    fsdp = lax.axis_index("fsdp")
    rollouts = queries.shape[0]
    low, high = keys_values[:, :, :HD], keys_values[:, :, HD:]
    holds_keys = seq < 4
    a = lax.ppermute(jnp.where(holds_keys, low, high), "seq", FIRST)
    b = lax.ppermute(jnp.where(holds_keys, high, low), "seq", SECOND)
    half = w_kv.shape[0] // 2
    w0, w1 = w_kv[:half], w_kv[half:]
    up0 = lax.ppermute(w0, "fsdp", X_UP)
    down1 = lax.ppermute(w1, "fsdp", X_DOWN)
    up1 = lax.ppermute(w1, "fsdp", X_UP)
    down0 = lax.ppermute(w0, "fsdp", X_DOWN)
    across0 = lax.ppermute(up0, "fsdp", X_UP)
    across1 = lax.ppermute(down1, "fsdp", X_DOWN)
    odd = (seq % 2).astype(jnp.int32).reshape(1)
    at = jnp.stack([fsdp // 4, fsdp % 4]).astype(jnp.int32)
    dq, gkv = attention(lengths, odd, queries, d_out, a, b)
    gkv = lax.all_to_all(gkv, "seq", split_axis=0, concat_axis=0, tiled=True)
    dq = lax.all_to_all(dq, "seq", split_axis=0, concat_axis=0, tiled=True)
    rows = rollouts * BAND
    g = gkv.reshape(N_SEQ, rows, 2, HD).transpose(1, 2, 0, 3).reshape(rows, 2 * N_SEQ * HD)
    g_near = lax.ppermute(g, "fsdp", NEAR)
    g_core = lax.ppermute(g, "fsdp", CORE)
    g_far = lax.ppermute(g_near, "fsdp", CORE)
    pieces = (g, g_core, g_near, g_far)
    blocks = []
    for weights in ((w_kv, up0, up1, down0, down1), (across0, across1)):
        own, core, near, far = project(pieces, weights)
        near = lax.ppermute(near, "fsdp", NEAR)
        far = lax.ppermute(far, "fsdp", DIAGONAL)
        core = lax.ppermute(core, "fsdp", CORE)
        blocks += [own, core, near, far]
    d_hidden = assemble(at, blocks).reshape(rollouts, BAND, -1)
    d_queries = dq.transpose(1, 2, 0, 3).reshape(rollouts, BAND, -1)
    return d_queries, d_hidden


def solution(mesh):
    in_specs = (
        P("fsdp", None, "seq"),
        P("fsdp", None, "seq"),
        P("fsdp", None, "seq"),
        P("fsdp"),
        P("fsdp", None),
    )
    out_specs = (P("fsdp", "seq", None), P("fsdp", "seq", None))
    return jax.shard_map(body, mesh=mesh, in_specs=in_specs, out_specs=out_specs, check_vma=False)
```

```python
import math

import jax
import jax.numpy as jnp
from jax import lax
from jax.experimental import pallas as pl
from jax.experimental.pallas import tpu as pltpu
from jax.sharding import PartitionSpec as P


HD = 128
GROUP = 8
N_SEQ = 8
BAND = 64
ROWS = N_SEQ * BAND
BI = 128
HEADS_A_STEP = 8
SCALE = 1.0 / math.sqrt(HD)
EXP2_SCALE = SCALE * math.log2(math.e)


def dot(a, b, ca, cb):
    return lax.dot_general(a, b, (((ca,), (cb,)), ((), ())), preferred_element_type=jnp.float32)


def attention_kernel(len_ref, odd_ref, q_ref, do_ref, a_ref, b_ref, stay_ref, c0_ref, c1_ref, gkv_ref, k_s, v_s, kt_s, dk_s, dv_s):
    step = pl.program_id(1)
    rollout = pl.program_id(0)
    live = len_ref[rollout]
    side = odd_ref[1]

    def put(block, head, value):
        value = value.reshape(BI // BAND, BAND, -1)
        cols = slice(head * HD, head * HD + value.shape[2])
        half, first = divmod(block * BI // BAND, N_SEQ // 2)
        bands = slice(first, first + BI // BAND)

        @pl.when(side == half)
        def _():
            stay_ref[bands, 0, :, cols] = value

        for r, ref in enumerate((c0_ref, c1_ref)):

            @pl.when((side != half) & (rollout == r))
            def _():
                ref[bands, :, cols] = value

    @pl.when(step == 0)
    def _():
        @pl.when(odd_ref[0] == 0)
        def _():
            k_s[...] = a_ref[0]
            v_s[...] = b_ref[0]

        @pl.when(odd_ref[0] != 0)
        def _():
            k_s[...] = b_ref[0]
            v_s[...] = a_ref[0]

        kt_s[...] = k_s[...].T
        dk_s[...] = jnp.zeros_like(dk_s)
        dv_s[...] = jnp.zeros_like(dv_s)

    def heads_of(ref, lo, hi):
        parts = [ref[0, lo:hi, head * HD : (head + 1) * HD] for head in range(HEADS_A_STEP)]
        return jnp.concatenate(parts, axis=0)

    for block in range(ROWS // BI):
        lo, hi = block * BI, (block + 1) * BI

        @pl.when(live > lo)
        def _():
            wide = HEADS_A_STEP * BI
            row = lax.broadcasted_iota(jnp.int32, (1, wide), 1) % BI
            below = lax.broadcasted_iota(jnp.int32, (BI, wide), 0) <= row
            q, do = heads_of(q_ref, lo, hi), heads_of(do_ref, lo, hi)
            spans = ([slice(0, lo)] if lo else []) + [slice(lo, hi)]
            scores = [dot(k_s[span, :], q, 1, 1) for span in spans]
            grad_prob = [dot(v_s[span, :], do, 1, 1) for span in spans]
            scores[-1] = jnp.where(below, scores[-1], -1e30)
            largest = scores[-1].max(0, keepdims=True)
            if lo:
                largest = jnp.maximum(largest, scores[0].max(0, keepdims=True))
            numer = [jnp.exp2((s - largest) * EXP2_SCALE) for s in scores]
            total = sum(n.sum(0, keepdims=True) for n in numer)
            inverse = jnp.where(lo + row < live, 1.0 / jnp.maximum(total, 1.0), 0.0)
            row_dot = sum((n * g).sum(0, keepdims=True) for n, g in zip(numer, grad_prob)) * inverse
            dqt = None
            for span, n, g in zip(spans, numer, grad_prob):
                prob = n * inverse
                grad_score = (prob * (g - row_dot)).astype(jnp.bfloat16)
                dv_s[span, :] += dot(prob.astype(jnp.bfloat16), do, 1, 0)
                dk_s[span, :] += dot(grad_score, q, 1, 0)
                part = dot(kt_s[:, span], grad_score, 1, 0)
                dqt = part if dqt is None else dqt + part
            dqt = dqt * SCALE
            dq = [dqt[:, head * BI : (head + 1) * BI].T.astype(jnp.bfloat16) for head in range(HEADS_A_STEP)]
            put(block, 0, jnp.concatenate(dq, axis=1))

        @pl.when(live <= lo)
        def _():
            put(block, 0, jnp.zeros((BI, HEADS_A_STEP * HD), jnp.bfloat16))

    @pl.when(step == pl.num_programs(1) - 1)
    def _():
        gkv_ref[:, 0, :, :HD] = (dk_s[...] * SCALE).astype(jnp.bfloat16).reshape(N_SEQ, BAND, HD)
        gkv_ref[:, 0, :, HD:] = dv_s[...].astype(jnp.bfloat16).reshape(N_SEQ, BAND, HD)


def attention(lengths, odd, queries, d_out, a, b):
    rollouts = queries.shape[0]
    wide = HEADS_A_STEP * HD
    rows = pl.BlockSpec((1, ROWS, wide), lambda r, h, *_: (r, 0, h))
    whole = pl.BlockSpec((1, ROWS, HD), lambda r, h, *_: (r, 0, 0))
    return pl.pallas_call(
        attention_kernel,
        out_shape=(
            jax.ShapeDtypeStruct((N_SEQ // 2, rollouts, BAND, GROUP * HD), jnp.bfloat16),
            jax.ShapeDtypeStruct((N_SEQ // 2, BAND, GROUP * HD), jnp.bfloat16),
            jax.ShapeDtypeStruct((N_SEQ // 2, BAND, GROUP * HD), jnp.bfloat16),
            jax.ShapeDtypeStruct((N_SEQ, rollouts, BAND, 2 * HD), jnp.bfloat16),
        ),
        grid_spec=pltpu.PrefetchScalarGridSpec(
            num_scalar_prefetch=2,
            grid=(rollouts, GROUP // HEADS_A_STEP),
            in_specs=[rows, rows, whole, whole],
            out_specs=[
                pl.BlockSpec((N_SEQ // 2, 1, BAND, wide), lambda r, h, *_: (0, r, 0, h)),
                pl.BlockSpec((N_SEQ // 2, BAND, wide), lambda r, h, *_: (0, 0, h)),
                pl.BlockSpec((N_SEQ // 2, BAND, wide), lambda r, h, *_: (0, 0, h)),
                pl.BlockSpec((N_SEQ, 1, BAND, 2 * HD), lambda r, h, *_: (0, r, 0, 0)),
            ],
            scratch_shapes=[
                pltpu.VMEM((ROWS, HD), jnp.bfloat16),
                pltpu.VMEM((ROWS, HD), jnp.bfloat16),
                pltpu.VMEM((HD, ROWS), jnp.bfloat16),
                pltpu.VMEM((ROWS, HD), jnp.float32),
                pltpu.VMEM((ROWS, HD), jnp.float32),
            ],
        ),
        name="attention",
    )(lengths, odd, queries, d_out, a, b)


def project_kernel(*refs):
    gs, outs, (g_s, w_s, sems) = refs[:2], refs[-5:-3], refs[-3:]
    weights = refs[2:-5]
    rows = gs[0].shape[0]
    starts = [sum(w.shape[0] for w in weights[:i]) for i in range(len(weights) + 1)]
    spans = [slice(a, b) for a, b in zip(starts, starts[1:])]
    loads = [pltpu.make_async_copy(g, g_s.at[i * rows : (i + 1) * rows], sems.at[i]) for i, g in enumerate(gs)]
    copies = [pltpu.make_async_copy(w, w_s.at[span], sems.at[2 + i]) for i, (w, span) in enumerate(zip(weights, spans))]
    for copy in loads + copies:
        copy.start()
    for copy in loads:
        copy.wait()
    for copy, span in zip(copies, spans):
        copy.wait()
        out = dot(g_s[...], w_s[span], 1, 1).astype(jnp.bfloat16)
        for k, o in enumerate(outs):
            o[:, span] = out[k * rows : (k + 1) * rows]


def project(pieces, weights):
    rows, depth = pieces[0].shape
    cols = sum(w.shape[0] for w in weights)
    stay = pl.BlockSpec(memory_space=pl.ANY)
    return pl.pallas_call(
        project_kernel,
        out_shape=(jax.ShapeDtypeStruct((rows, cols), jnp.bfloat16),) * 2,
        in_specs=[stay] * (2 + len(weights)),
        out_specs=[pl.BlockSpec(memory_space=pltpu.VMEM)] * 2,
        scratch_shapes=[
            pltpu.VMEM((2 * rows, depth), jnp.bfloat16),
            pltpu.VMEM((cols, depth), jnp.bfloat16),
            pltpu.SemaphoreType.DMA((2 + len(weights),)),
        ],
        compiler_params=pltpu.CompilerParams(vmem_limit_bytes=20 << 20),
        name="project",
    )(*pieces, *weights)


def assemble_kernel(at_ref, *refs):
    x, q = at_ref[0], at_ref[1]
    o_ref = refs[-1]
    for block, (k, pieces) in zip(refs, BLOCKS):
        start = 0
        for step, first, width in pieces:
            col = pl.multiple_of(((x + step) % 4 * 4 + (q ^ k)) * SHARD + first, HALF)
            o_ref[:, pl.ds(col, width)] = block[:, start : start + width]
            start += width


def assemble(at, blocks):
    rows = blocks[0].shape[0]
    cols = sum(block.shape[1] for block in blocks)
    vmem = pl.BlockSpec(memory_space=pltpu.VMEM)
    return pl.pallas_call(
        assemble_kernel,
        out_shape=jax.ShapeDtypeStruct((rows, cols), jnp.bfloat16),
        in_specs=[pl.BlockSpec(memory_space=pltpu.SMEM)] + [vmem] * len(blocks),
        out_specs=vmem,
        compiler_params=pltpu.CompilerParams(vmem_limit_bytes=16 << 20),
        name="assemble",
    )(at, *blocks)


X_UP = [(f, (f + 4) % 16) for f in range(16)]
X_DOWN = [(f, (f + 12) % 16) for f in range(16)]
CORE = [(f, f ^ 1) for f in range(16)]
NEAR = [(f, f ^ 2) for f in range(16)]
DIAGONAL = [(f, f ^ 3) for f in range(16)]
SHARD, HALF = 512, 256
THREE = ((0, 0, SHARD), (3, 0, SHARD), (1, 0, SHARD))
EARLY = ((0, 0, SHARD), (3, 0, HALF), (1, HALF, HALF))
LATE = ((3, HALF, HALF), (1, 0, HALF), (2, 0, SHARD))
BLOCKS = ((0, EARLY), (1, EARLY), (2, THREE), (3, THREE), (2, ((2, 0, SHARD),)), (3, ((2, 0, SHARD),)), (0, LATE), (1, LATE))
OTHER_HALF = [(s, s ^ 4) for s in range(8)]
HALVES = [[0, 1, 2, 3], [4, 5, 6, 7]]
FIRST = [(t, 2 * t) for t in range(4)] + [(4 + t, 2 * t + 1) for t in range(4)]
SECOND = [(t, 2 * t + 1) for t in range(4)] + [(4 + t, 2 * t) for t in range(4)]


def body(queries, d_out, keys_values, lengths, w_kv):
    seq = lax.axis_index("seq")
    fsdp = lax.axis_index("fsdp")
    rollouts = queries.shape[0]
    low, high = keys_values[:, :, :HD], keys_values[:, :, HD:]
    holds_keys = seq < 4
    a = lax.ppermute(jnp.where(holds_keys, low, high), "seq", FIRST)
    b = lax.ppermute(jnp.where(holds_keys, high, low), "seq", SECOND)
    half = w_kv.shape[0] // 2
    w0, w1 = w_kv[:half], w_kv[half:]
    up0 = lax.ppermute(w0, "fsdp", X_UP)
    down1 = lax.ppermute(w1, "fsdp", X_DOWN)
    up1 = lax.ppermute(w1, "fsdp", X_UP)
    down0 = lax.ppermute(w0, "fsdp", X_DOWN)
    across0 = lax.ppermute(up0, "fsdp", X_UP)
    across1 = lax.ppermute(down1, "fsdp", X_DOWN)
    odd = jnp.stack([seq % 2, seq // 4]).astype(jnp.int32)
    at = jnp.stack([fsdp // 4, fsdp % 4]).astype(jnp.int32)
    stay, c0, c1, gkv = attention(lengths, odd, queries, d_out, a, b)
    gkv = lax.all_to_all(gkv, "seq", split_axis=0, concat_axis=0, tiled=True)
    c0 = lax.ppermute(c0, "seq", OTHER_HALF)
    c1 = lax.ppermute(c1, "seq", OTHER_HALF)
    stay = lax.all_to_all(stay, "seq", 0, 0, axis_index_groups=HALVES, tiled=True)
    cross = jnp.stack([c0, c1], axis=1)
    cross = lax.all_to_all(cross, "seq", 0, 0, axis_index_groups=HALVES, tiled=True)
    rows = rollouts * BAND
    g = gkv.reshape(N_SEQ, rows, 2, HD).transpose(1, 2, 0, 3).reshape(rows, 2 * N_SEQ * HD)
    g_near = lax.ppermute(g, "fsdp", NEAR)
    g_core = lax.ppermute(g, "fsdp", CORE)
    g_far = lax.ppermute(g_near, "fsdp", CORE)
    own, core = project((g, g_core), (w_kv, up0, down1))
    core = lax.ppermute(core, "fsdp", CORE)
    blocks = [own, core]
    for weights in ((w_kv, up0, up1, down0, down1), (across0, across1)):
        near, far = project((g_near, g_far), weights)
        near = lax.ppermute(near, "fsdp", NEAR)
        far = lax.ppermute(far, "fsdp", DIAGONAL)
        blocks += [near, far]
    own, core = project((g, g_core), (up1, down0, across0, across1))
    core = lax.ppermute(core, "fsdp", CORE)
    blocks += [own, core]
    d_hidden = assemble(at, blocks).reshape(rollouts, BAND, -1)
    dq = jnp.where(seq < 4, jnp.concatenate([stay, cross]), jnp.concatenate([cross, stay]))
    d_queries = dq.transpose(1, 2, 0, 3).reshape(rollouts, BAND, -1)
    return d_queries, d_hidden


def solution(mesh):
    in_specs = (
        P("fsdp", None, "seq"),
        P("fsdp", None, "seq"),
        P("fsdp", None, "seq"),
        P("fsdp"),
        P("fsdp", None),
    )
    out_specs = (P("fsdp", "seq", None), P("fsdp", "seq", None))
    return jax.shard_map(body, mesh=mesh, in_specs=in_specs, out_specs=out_specs, check_vma=False)
```
